32 devices in a mesh: ep: 8 (over y, x, core), tp: 4 (over z).
Axes of the slice: x: 2, y: 2, z: 4, core: 2. Of those that a mesh axis runs over, the one named last changes fastest.
Arguments:
- latents: bfloat16 [64, 1024], P('ep'), may hold values from -6 to 6
- expert_ids: int32 [64, 22], P('ep'), may hold values from 0 to 127, all different within a row; in each aligned block of 8 rows (0 to 7, 8 to 15, ...) at most 3 rows name the same one
- gate_values: float32 [64, 22], P('ep'), may hold values from 0.05 to 0.5
- w_up: bfloat16 [128, 1024, 2688], P('ep', None, 'tp'), may hold values from -0.1875 to 0.1875
- w_down: bfloat16 [128, 2688, 1024], P('ep', 'tp'), may hold values from -0.125 to 0.125
Outputs:
- mixed_rows: bfloat16 [64, 1024], P('ep', 'tp')
The draws below stay inside these ranges and needn't reach their ends.
Inputs may be any that keep to these rules, and one draw needn't show every extreme that they name: `expert_ids`: each row names 22 different experts. Among the 8 tokens of one index of ep no expert is named more than 3 times, a bound that some block reaches.
All inputs are finite; a program needn't handle non-finite values.
Results may differ from the reference program's by a relative error of at most 0.014.
Values may be sent and summed in bfloat16 or wider, within the bound.
No kernel may reach another device: no remote copies, remote signals or barrier semaphores. Data moves between devices by JAX's collectives and lax.ppermute only.
A program may use at most 128 MiB of HBM per device.

```python
import math
import jax
import jax.numpy as jnp
import numpy as np
from jax import lax

L = 1024
FF = 2688
TOP = 22
EXPERTS = 128
TOK_DEV = 8
MOST = 3
TOKENS = 64
N_EP = 8


def block_levels(stream_key, dims, shards, low, top_value):
    def one(axis_at, blocks):
        draws = jax.random.uniform(jax.random.fold_in(jax.random.fold_in(stream_key, 6), axis_at), (blocks,), jnp.float32, low / len(shards), top_value / len(shards))
        return jnp.repeat(jnp.exp(draws), dims[axis_at] // blocks).reshape((-1,) + (1,) * (len(dims) - axis_at - 1))

    level = one(*shards[0])
    for cut in shards[1:]:
        level = level * one(*cut)
    return level


def shared_out(rng, own, number, rows, amount, top, bound, slope):
    ranking = jax.random.permutation(rng, amount)
    heavy_load, common = load_shares(amount, rows * top, bound, slope, True), load_shares(amount, rows * top, bound, slope, False)
    places = jnp.arange(amount)

    def named(sizes, turn):
        used = int((sizes > 0).sum())
        fixed = max(1, used // 4)
        shifted = fixed + (places - fixed + turn * (used - fixed)) % max(1, amount - fixed)
        return jnp.zeros((amount,), jnp.int32).at[ranking[jnp.where(places < fixed, places, shifted)]].set(jnp.asarray(sizes, jnp.int32))

    sizes = jnp.where(number % 4 == 0, named(heavy_load, number // 4), named(common, number - number // 4 - 1))
    mixed = jax.random.permutation(jax.random.fold_in(own, 3), amount)
    giver, taker = mixed[0:amount // 2 * 2:2], mixed[1:amount // 2 * 2:2]
    margin = jnp.minimum(sizes[giver] - 1, bound - sizes[taker]) // 2
    margin = jnp.where((giver == ranking[0]) | (taker == ranking[0]) | (sizes[taker] == 0), 0, jnp.maximum(margin, 0))
    shifted = jax.random.randint(jax.random.fold_in(own, 4), (amount // 2,), 0, 1 << 20) % (margin + 1)
    sizes = sizes.at[giver].add(-shifted).at[taker].add(shifted)
    labels = jnp.searchsorted(jnp.cumsum(sizes), jnp.arange(rows * top), side="right").astype(jnp.int32)
    grid = labels.reshape(top, rows).T
    grid = grid[jax.random.permutation(jax.random.fold_in(own, 1), rows)]
    turn = jax.random.randint(jax.random.fold_in(own, 2), (rows, 1), 0, top)
    return jnp.take_along_axis(grid, (jnp.arange(top)[None, :] + turn) % top, axis=1)


def load_shares(number_of, total, most, slope, full):
    weights = [(1 << 20) // math.isqrt(standing ** slope) + 1 for standing in range(1, number_of + 1)]
    largest = most if full else min(most, max(-(-total // number_of), total * weights[0] // sum(weights)))
    least = 1 if total - largest >= number_of - 1 else 0
    given, surplus = [largest] + [least] * (number_of - 1), total - largest - least * (number_of - 1)
    while surplus > 0:
        movable = [i for i in range(1, number_of) if given[i] < largest] or [i for i in range(1, number_of) if given[i] < most]
        mass, budget = sum([weights[i] for i in movable]), surplus
        for i in movable:
            more = min(most - given[i], max(1, budget * weights[i] // mass), surplus)
            given[i] = given[i] + more
            surplus = surplus - more
    return np.array(given)


def centred(key, extent, scale, limit, shards=(), held_as=jnp.bfloat16):
    level = block_levels(key, extent, shards, -0.22, 0.18) if shards else 1.0
    result = jax.random.normal(key, extent, jnp.float32) * scale * level
    return jnp.minimum(jnp.maximum(result, -limit), limit).astype(held_as)


def setup_inputs(seed: int = 0) -> dict:
    streams_of = jax.random.split(jax.random.key(seed), 6)
    latents = centred(streams_of[0], (TOKENS, L), 1.0, 6.0, ((0, 8),))
    expert_ids_keys = jax.random.split(jax.random.fold_in(streams_of[1], 1), TOKENS // TOK_DEV)
    expert_ids_turns = jax.random.permutation(jax.random.fold_in(streams_of[1], 3), TOKENS // TOK_DEV)
    expert_ids = jax.vmap(lambda own, number: shared_out(jax.random.fold_in(streams_of[1], 2), own, number, TOK_DEV, EXPERTS, TOP, MOST, 2))(expert_ids_keys, expert_ids_turns).reshape((TOKENS, TOP))
    gate_values = jnp.clip(jnp.exp(math.log(0.5) - 2.3025851 * jax.random.uniform(streams_of[2], (TOKENS, TOP), jnp.float32) ** block_levels(streams_of[2], (TOKENS, TOP), ((0, 8),), -0.2, 0.2)), 0.05, 0.5)
    w_up = centred(streams_of[3], (EXPERTS, L, FF), L ** -0.5, 0.1875, ((0, 8), (2, 4)))
    w_down = centred(streams_of[4], (EXPERTS, FF, L), FF ** -0.5, 0.125, ((0, 8), (1, 4)))
    return {"latents": latents, "expert_ids": expert_ids, "gate_values": gate_values, "w_up": w_up, "w_down": w_down}


def reference(latents, expert_ids, gate_values, w_up, w_down):
    token_total = expert_ids.shape[0]
    model_width = latents.shape[1]
    slot_most = 3 * TOK_DEV // 8
    capacity = N_EP * slot_most
    block_ids = jnp.arange(token_total, dtype=jnp.int32) // TOK_DEV

    def one_expert(running, inputs):
        up_matrix, down_matrix, expert = inputs
        chosen = expert_ids == expert
        named_count = jnp.sum(chosen.astype(jnp.int32), axis=1)
        blocked = named_count.reshape(N_EP, TOK_DEV)
        before = (jnp.cumsum(blocked, axis=1) - blocked).reshape(token_total)
        target = jnp.where(named_count > 0, block_ids * slot_most + before, capacity).astype(jnp.int32)
        gathered = jnp.zeros((capacity + 1, model_width), jnp.bfloat16).at[target].set(latents)[:capacity]
        preact = jnp.dot(gathered, up_matrix, preferred_element_type=jnp.float32)
        hidden = jnp.square(jnp.maximum(preact, 0.0)).astype(jnp.bfloat16)
        expert_out = jnp.dot(hidden, down_matrix, preferred_element_type=jnp.float32).astype(jnp.bfloat16)
        expert_out = lax.optimization_barrier(expert_out)
        padded = jnp.concatenate([expert_out, jnp.zeros((1, model_width), jnp.bfloat16)], axis=0)
        picked = padded[target].astype(jnp.float32)
        weight = jnp.sum(jnp.where(chosen, gate_values, jnp.zeros_like(gate_values)), axis=1)
        return running + weight[:, None] * picked, None

    start_sum = jnp.zeros((token_total, model_width), jnp.float32)
    experts_seq = jnp.arange(w_up.shape[0], dtype=jnp.int32)
    total = lax.scan(one_expert, start_sum, (w_up, w_down, experts_seq))[0]
    return total.astype(jnp.bfloat16)
```

```python
import functools

import jax
import jax.numpy as jnp
from jax import lax
from jax.experimental import pallas as pl
from jax.experimental.pallas import tpu as pltpu
from jax.sharding import PartitionSpec as P


NT = (((1,), (1,)), ((), ()))
TN = (((0,), (0,)), ((), ()))
VMEM = pl.BlockSpec(memory_space=pltpu.VMEM)
HBM = pl.BlockSpec(memory_space=pltpu.HBM)
DIRECT = 8


def pack_kernel(expert_total, latents_hbm, ids_hbm, gates_hbm, packed, ids, gates, sems):
    tokens, width = latents_hbm.shape
    copies = [
        pltpu.make_async_copy(ids_hbm, ids, sems.at[0]),
        pltpu.make_async_copy(gates_hbm, gates, sems.at[1]),
        pltpu.make_async_copy(latents_hbm, packed.at[:, :width], sems.at[2]),
    ]
    for copy in copies:
        copy.start()
    copies[0].wait()
    copies[1].wait()
    lanes = lax.broadcasted_iota(jnp.int32, (tokens, expert_total), 1)
    dense = jnp.zeros((tokens, expert_total), jnp.float32)
    for k in range(ids.shape[1]):
        dense += jnp.where(ids[:, k : k + 1] == lanes, gates[:, k : k + 1], 0.0)
    lead = dense.astype(jnp.bfloat16)
    packed[:, width : width + expert_total] = lead
    packed[:, width + expert_total :] = (dense - lead.astype(jnp.float32)).astype(jnp.bfloat16)
    copies[2].wait()


def load_kernel(rows_hbm, rows, sems):
    copies = [
        pltpu.make_async_copy(rows_hbm.at[e], rows.at[e], sems.at[e]) for e in range(rows.shape[0])
    ]
    for copy in copies:
        copy.start()
    for copy in copies:
        copy.wait()


def expert_kernel(flips, own, other, up_head, up_hbm, down_hbm, partial, up_tail, down_rows, packed, hidden, total, sems):
    experts, units, width = down_hbm.shape
    head = up_head.shape[0]
    tokens = packed.shape[0]
    expert_total = (packed.shape[1] - width) // 2
    up_copies = [
        pltpu.make_async_copy(up_hbm.at[e], up_tail.at[e - head], sems.at[0, e])
        for e in range(head, experts)
    ]
    down_copies = [
        pltpu.make_async_copy(down_hbm.at[e], down_rows.at[e], sems.at[1, e])
        for e in range(experts)
    ]
    for copy in up_copies + down_copies:
        copy.start()
    packed[: own.shape[0]] = own[...]
    packed[own.shape[0] :] = other[...]
    me = lax.axis_index("ep")
    shape = (max(8, experts), expert_total)
    pick = lax.broadcasted_iota(jnp.int32, shape, 1) == (
        me * experts + lax.broadcasted_iota(jnp.int32, shape, 0)
    )
    pick = pick.astype(jnp.bfloat16)
    weights = lax.dot_general(
        pick, packed[:, width : width + expert_total], NT, preferred_element_type=jnp.float32
    ) + lax.dot_general(
        pick, packed[:, width + expert_total :], NT, preferred_element_type=jnp.float32
    )
    x = packed[:, :width]
    for e in range(experts):
        if e >= head:
            up_copies[e - head].wait()
        rows = up_head[e] if e < head else up_tail[e - head]
        preact = lax.dot_general(rows, x, NT, preferred_element_type=jnp.float32)
        scaled = jnp.square(jnp.maximum(preact, 0.0)) * weights[e : e + 1, :]
        hidden[e] = scaled.astype(jnp.bfloat16)
    step = max(1, experts // 8)
    for e in range(0, experts, step):
        for copy in down_copies[e : e + step]:
            copy.wait()
        term = lax.dot_general(
            hidden[e : e + step].reshape(step * units, tokens),
            down_rows[e : e + step].reshape(step * units, width),
            TN,
            preferred_element_type=jnp.float32,
        )
        if e == 0:
            total[...] = term
        else:
            total[...] += term
    _, block_rows, quarter = partial.shape
    quarters = width // quarter
    for block in range(tokens // block_rows):
        place = block if flips is None else me ^ flips[block]
        for q in range(quarters):
            partial[place * quarters + q] = total[
                block * block_rows : (block + 1) * block_rows, q * quarter : (q + 1) * quarter
            ].astype(jnp.bfloat16)


def per_device(latents, expert_ids, gate_values, w_up, w_down):
    ep_count = lax.axis_size("ep")
    tp_count = lax.axis_size("tp")
    token_count, model_width = latents.shape
    experts, _, units = w_up.shape
    expert_total = experts * ep_count
    tokens = token_count * ep_count
    packed_width = model_width + 2 * expert_total
    up_rows = pltpu.with_memory_space_constraint(jnp.swapaxes(w_up, 1, 2), pltpu.HBM)
    down_rows = pltpu.with_memory_space_constraint(w_down, pltpu.HBM)
    head = max(1, experts * 5 // 8)
    row_bytes = 2 * units * model_width
    packed = pl.pallas_call(
        functools.partial(pack_kernel, expert_total),
        out_shape=jax.ShapeDtypeStruct((token_count, packed_width), jnp.bfloat16),
        in_specs=[HBM] * 3,
        out_specs=VMEM,
        scratch_shapes=[
            pltpu.VMEM(expert_ids.shape, jnp.int32),
            pltpu.VMEM(gate_values.shape, jnp.float32),
            pltpu.SemaphoreType.DMA((3,)),
        ],
        compiler_params=pltpu.CompilerParams(vmem_limit_bytes=2 << 20),
    )(*(pltpu.with_memory_space_constraint(a, pltpu.HBM) for a in (latents, expert_ids, gate_values)))

    def swap(rows, flip):
        return lax.ppermute(rows, "ep", [(i, i ^ flip) for i in range(ep_count)])

    direct = ep_count <= DIRECT
    chips = list(range(0, ep_count, 2))
    pieces = [packed]
    for s in chips[1:] if direct else ():
        pieces.append(swap(packed, s))
    up_head = pl.pallas_call(
        load_kernel,
        out_shape=pltpu.VMEM((head, units, model_width), jnp.bfloat16),
        in_specs=[HBM],
        out_specs=VMEM,
        scratch_shapes=[pltpu.SemaphoreType.DMA((head,))],
        compiler_params=pltpu.CompilerParams(vmem_limit_bytes=1 << 20),
        cost_estimate=pl.CostEstimate(flops=0, bytes_accessed=head * row_bytes, transcendentals=0),
    )(up_rows)
    if direct:
        own = jnp.concatenate(pieces)
        other = swap(own, 1)
        flips = chips + [s + 1 for s in chips]
    else:
        own, other = jnp.split(lax.all_gather(packed, "ep", axis=0, tiled=True), 2)
        flips = None
    partial = pl.pallas_call(
        functools.partial(expert_kernel, flips),
        out_shape=jax.ShapeDtypeStruct(
            (ep_count * tp_count, token_count, model_width // tp_count), jnp.bfloat16
        ),
        in_specs=[VMEM, VMEM, VMEM, HBM, HBM],
        out_specs=VMEM,
        scratch_shapes=[
            pltpu.VMEM((max(1, experts - head), units, model_width), jnp.bfloat16),
            pltpu.VMEM((experts, units, model_width), jnp.bfloat16),
            pltpu.VMEM((tokens, packed_width), jnp.bfloat16),
            pltpu.VMEM((experts, units, tokens), jnp.bfloat16),
            pltpu.VMEM((tokens, model_width), jnp.float32),
            pltpu.SemaphoreType.DMA((2, experts)),
        ],
        compiler_params=pltpu.CompilerParams(
            vmem_limit_bytes=(2 * experts - head) * row_bytes + (8 << 20)
            + 8 * tokens * packed_width
        ),
        cost_estimate=pl.CostEstimate(
            flops=4 * tokens * experts * units * model_width,
            bytes_accessed=(2 * experts - head) * row_bytes,
            transcendentals=0,
        ),
    )(own, other, up_head, up_rows, down_rows)
    received = lax.all_to_all(partial, ("ep", "tp"), split_axis=0, concat_axis=0, tiled=True)
    return jnp.sum(received.astype(jnp.float32), axis=0).astype(jnp.bfloat16)


def solution(mesh):
    return jax.shard_map(
        per_device,
        mesh=mesh,
        in_specs=(
            P("ep", None),
            P("ep", None),
            P("ep", None),
            P("ep", None, "tp"),
            P("ep", "tp", None),
        ),
        out_specs=P("ep", "tp"),
        check_vma=False,
    )
```

```python
import functools

import jax
import jax.numpy as jnp
from jax import lax
from jax.experimental import pallas as pl
from jax.experimental.pallas import tpu as pltpu
from jax.sharding import PartitionSpec as P


NT = (((1,), (1,)), ((), ()))
TN = (((0,), (0,)), ((), ()))
VMEM = pl.BlockSpec(memory_space=pltpu.VMEM)
HBM = pl.BlockSpec(memory_space=pltpu.HBM)
DIRECT = 8


def pack_kernel(expert_total, latents_hbm, ids_hbm, gates_hbm, packed, ids, gates, sems):
    tokens, width = latents_hbm.shape
    copies = [
        pltpu.make_async_copy(ids_hbm, ids, sems.at[0]),
        pltpu.make_async_copy(gates_hbm, gates, sems.at[1]),
        pltpu.make_async_copy(latents_hbm, packed.at[:, :width], sems.at[2]),
    ]
    for copy in copies:
        copy.start()
    copies[0].wait()
    copies[1].wait()
    lanes = lax.broadcasted_iota(jnp.int32, (tokens, expert_total), 1)
    dense = jnp.zeros((tokens, expert_total), jnp.float32)
    for k in range(ids.shape[1]):
        dense += jnp.where(ids[:, k : k + 1] == lanes, gates[:, k : k + 1], 0.0)
    lead = dense.astype(jnp.bfloat16)
    packed[:, width : width + expert_total] = lead
    packed[:, width + expert_total :] = (dense - lead.astype(jnp.float32)).astype(jnp.bfloat16)
    copies[2].wait()


def load_kernel(rows_hbm, rows, sems):
    copies = [
        pltpu.make_async_copy(rows_hbm.at[e], rows.at[e], sems.at[e]) for e in range(rows.shape[0])
    ]
    for copy in copies:
        copy.start()
    for copy in copies:
        copy.wait()


def expert_kernel(flips, *refs):
    *pieces, up_head, up_hbm, down_hbm, partial = refs[:-6]
    up_tail, down_rows, packed, hidden, total, sems = refs[-6:]
    experts, units, width = down_hbm.shape
    head = up_head.shape[0]
    tokens = packed.shape[0]
    expert_total = (packed.shape[1] - width) // 2

    def up_copy(e):
        return pltpu.make_async_copy(up_hbm.at[e], up_tail.at[e - head], sems.at[0, e])

    def down_copy(e):
        return pltpu.make_async_copy(down_hbm.at[e], down_rows.at[e], sems.at[1, e])

    @pl.loop(head, experts)
    def _(e):
        up_copy(e).start()

    @pl.loop(0, experts)
    def _(e):
        down_copy(e).start()

    each = pieces[0].shape[0]
    for i, piece in enumerate(pieces):
        packed[i * each : (i + 1) * each] = piece[...]
    me = lax.axis_index("ep")
    shape = (max(8, experts), expert_total)
    pick = lax.broadcasted_iota(jnp.int32, shape, 1) == (
        me * experts + lax.broadcasted_iota(jnp.int32, shape, 0)
    )
    pick = pick.astype(jnp.bfloat16)
    weights = lax.dot_general(
        pick, packed[:, width : width + expert_total], NT, preferred_element_type=jnp.float32
    ) + lax.dot_general(
        pick, packed[:, width + expert_total :], NT, preferred_element_type=jnp.float32
    )
    x = packed[:, :width]
    for e in range(experts):
        if e == head:
            for i in range(head, experts):
                up_copy(i).wait()
        rows = up_head[e] if e < head else up_tail[e - head]
        preact = lax.dot_general(rows, x, NT, preferred_element_type=jnp.float32)
        scaled = jnp.square(jnp.maximum(preact, 0.0)) * weights[e : e + 1, :]
        hidden[e] = scaled.astype(jnp.bfloat16)
    step = max(1, experts // 8)
    for e in range(0, experts, step):
        for i in range(e, e + step):
            down_copy(i).wait()
        term = lax.dot_general(
            hidden[e : e + step].reshape(step * units, tokens),
            down_rows[e : e + step].reshape(step * units, width),
            TN,
            preferred_element_type=jnp.float32,
        )
        if e == 0:
            total[...] = term
        else:
            total[...] += term
    _, block_rows, quarter = partial.shape
    quarters = width // quarter
    for block in range(tokens // block_rows):
        place = block if flips is None else me ^ flips[block]
        for q in range(quarters):
            partial[place * quarters + q] = total[
                block * block_rows : (block + 1) * block_rows, q * quarter : (q + 1) * quarter
            ].astype(jnp.bfloat16)


def per_device(latents, expert_ids, gate_values, w_up, w_down):
    ep_count = lax.axis_size("ep")
    tp_count = lax.axis_size("tp")
    token_count, model_width = latents.shape
    experts, _, units = w_up.shape
    expert_total = experts * ep_count
    tokens = token_count * ep_count
    packed_width = model_width + 2 * expert_total
    up_rows = pltpu.with_memory_space_constraint(jnp.swapaxes(w_up, 1, 2), pltpu.HBM)
    down_rows = pltpu.with_memory_space_constraint(w_down, pltpu.HBM)
    head = max(1, experts * 5 // 8)
    row_bytes = 2 * units * model_width
    packed = pl.pallas_call(
        functools.partial(pack_kernel, expert_total),
        out_shape=jax.ShapeDtypeStruct((token_count, packed_width), jnp.bfloat16),
        in_specs=[HBM] * 3,
        out_specs=VMEM,
        scratch_shapes=[
            pltpu.VMEM(expert_ids.shape, jnp.int32),
            pltpu.VMEM(gate_values.shape, jnp.float32),
            pltpu.SemaphoreType.DMA((3,)),
        ],
        compiler_params=pltpu.CompilerParams(vmem_limit_bytes=2 << 20),
    )(*(pltpu.with_memory_space_constraint(a, pltpu.HBM) for a in (latents, expert_ids, gate_values)))

    def swap(rows, flip):
        return lax.ppermute(rows, "ep", [(i, i ^ flip) for i in range(ep_count)])

    direct = ep_count <= DIRECT
    chips = list(range(0, ep_count, 2))
    if direct:
        pieces = [jnp.concatenate([packed, swap(packed, 1)])]
        for s in chips[1:]:
            pieces.append(swap(pieces[0], s))
        flips = [s + core for s in chips for core in range(2)]
    else:
        pieces = [lax.all_gather(packed, "ep", axis=0, tiled=True)]
        flips = None
    up_head = pl.pallas_call(
        load_kernel,
        out_shape=pltpu.VMEM((head, units, model_width), jnp.bfloat16),
        in_specs=[HBM],
        out_specs=VMEM,
        scratch_shapes=[pltpu.SemaphoreType.DMA((head,))],
        compiler_params=pltpu.CompilerParams(vmem_limit_bytes=1 << 20),
        cost_estimate=pl.CostEstimate(flops=0, bytes_accessed=head * row_bytes, transcendentals=0),
    )(up_rows)
    partial = pl.pallas_call(
        functools.partial(expert_kernel, flips),
        out_shape=jax.ShapeDtypeStruct(
            (ep_count * tp_count, token_count, model_width // tp_count), jnp.bfloat16
        ),
        in_specs=[VMEM] * (len(pieces) + 1) + [HBM] * 2,
        out_specs=VMEM,
        scratch_shapes=[
            pltpu.VMEM((max(1, experts - head), units, model_width), jnp.bfloat16),
            pltpu.VMEM((experts, units, model_width), jnp.bfloat16),
            pltpu.VMEM((tokens, packed_width), jnp.bfloat16),
            pltpu.VMEM((experts, units, tokens), jnp.bfloat16),
            pltpu.VMEM((tokens, model_width), jnp.float32),
            pltpu.SemaphoreType.DMA((2, experts)),
        ],
        compiler_params=pltpu.CompilerParams(
            vmem_limit_bytes=(2 * experts - head) * row_bytes + (8 << 20)
            + 8 * tokens * packed_width
        ),
        cost_estimate=pl.CostEstimate(
            flops=4 * tokens * experts * units * model_width,
            bytes_accessed=(2 * experts - head) * row_bytes,
            transcendentals=0,
        ),
    )(*pieces, up_head, up_rows, down_rows)
    received = lax.all_to_all(partial, ("ep", "tp"), split_axis=0, concat_axis=0, tiled=True)
    return jnp.sum(received.astype(jnp.float32), axis=0).astype(jnp.bfloat16)


def solution(mesh):
    return jax.shard_map(
        per_device,
        mesh=mesh,
        in_specs=(
            P("ep", None),
            P("ep", None),
            P("ep", None),
            P("ep", None, "tp"),
            P("ep", "tp", None),
        ),
        out_specs=P("ep", "tp"),
        check_vma=False,
    )
```
